512 devices in a mesh: lon: 64 (over z_lo, y, core), plane: 8 (over z_hi, x).
Axes of the slice: x: 4, y: 8, z: 8 (z_hi: 2, z_lo: 4; z = z_hi * 4 + z_lo), core: 2. Of those that a mesh axis runs over, the one named last changes fastest.
Arguments:
- potential: float32 [8, 256, 16384], P('plane', None, 'lon'), may hold values from -0.6 to 0.6
- lens_weight: float32 [8, 8], P('plane'), may hold values from 0.1 to 0.3
- cycle_shift: int32 [2, 256], replicated, may hold values from -3 to 2
- cycle_weight: int32 [2, 256], replicated, may hold values from 0 to 16
- cycle_scale: float32 [256], replicated, may hold values from 1 to 2
Outputs:
- displacement: float32 [8, 2, 256, 16384], P('plane', None, None, 'lon')
- jacobian: float32 [8, 4, 256, 16384], P('plane', None, None, 'lon')
The draws below stay inside these ranges and needn't reach their ends.
All inputs are finite; a program needn't handle non-finite values.
Results may differ from the reference program's by a relative error of at most 0.00002.
Values sent between devices are 32-bit elements; how exact they have to be, the bound alone decides.
No kernel may reach another device: no remote copies, remote signals or barrier semaphores. Data moves between devices by JAX's collectives and lax.ppermute only.
A program may use at most 64 MiB of HBM per device.

```python
import math
import jax
import jax.numpy as jnp
from jax import lax

ROWS = 256
NLON = 16384
PLANES = 8
SOURCES = 8


def set_ends(array, key, least, largest):
    shape = array.shape
    index_at = [jax.random.randint(jax.random.fold_in(key, axis), (), 0, shape[axis]) for axis in range(len(shape))]
    array = array.at[tuple(index_at)].set(least)
    longest = shape.index(max(shape))
    index_at[longest] = (index_at[longest] + 1) % shape[longest]
    return array.at[tuple(index_at)].set(largest)


def block_scale(own_key, shape, shards, smallest, high):
    level, own = 1.0, jax.random.fold_in(own_key, 6)
    for axis_at, blocks in shards:
        heights = jnp.exp(jax.random.uniform(jax.random.fold_in(own, axis_at), (blocks,), jnp.float32, smallest / len(shards), high / len(shards)))
        level = level * jnp.repeat(heights, shape[axis_at] // blocks).reshape([-1 if axis == axis_at else 1 for axis in range(len(shape))])
    return level


def gaussian(key, dims, deviation, bound, split=(), kind=jnp.bfloat16):
    loudness = block_scale(key, dims, split, -0.22, 0.18) if split else 1.0
    values = jax.random.normal(key, dims, jnp.float32) * deviation * loudness
    return jnp.minimum(jnp.maximum(values, -bound), bound).astype(kind)


def setup_inputs(seed: int = 0) -> dict:
    streams_of = jax.random.split(jax.random.key(seed), 6)
    potential = gaussian(streams_of[0], (PLANES, ROWS, NLON), 0.1, 0.6, ((0, 8), (2, 64)), jnp.float32)
    lens_weight = jnp.clip(0.1 + 0.20000001043081284 * jax.random.uniform(streams_of[1], (SOURCES, PLANES), jnp.float32) ** block_scale(streams_of[1], (SOURCES, PLANES), ((0, 8),), -0.2, 0.2), 0.1, 0.3)
    cycle_shift = set_ends(jax.random.randint(streams_of[2], (2, ROWS), -3, 3), jax.random.fold_in(streams_of[2], 1), -3, 2).astype(jnp.int32)
    cycle_weight = set_ends(jax.random.randint(streams_of[3], (2, ROWS), 0, 17), jax.random.fold_in(streams_of[3], 1), 0, 16).astype(jnp.int32)
    cycle_scale = jnp.clip(jnp.exp(jax.random.uniform(streams_of[4], (ROWS,), jnp.float32, math.log(1.0), math.log(2.0))), 1.0, 2.0)
    return {"potential": potential, "lens_weight": lens_weight, "cycle_shift": cycle_shift, "cycle_weight": cycle_weight, "cycle_scale": cycle_scale}


def cycle_interp(row_block, shifts, weights, offset, total):
    columns = jnp.arange(total, dtype=jnp.int32)
    index = (columns[None, :] + shifts[:, None].astype(jnp.int32) + offset) % total
    picked = jnp.take_along_axis(row_block, index, axis=1)
    index_next = (index + 1) % total
    picked_next = jnp.take_along_axis(row_block, index_next, axis=1)
    frac = weights.astype(jnp.float32)[:, None] / 16.0
    return (1.0 - frac) * picked + frac * picked_next


def derivatives(field, cycle_shift, cycle_weight, cycle_scale):
    total = field.shape[1]
    padded = jnp.pad(field, ((1, 1), (0, 0)))
    north_rows = padded[:-2]
    south_rows = padded[2:]
    north = [cycle_interp(north_rows, cycle_shift[0], cycle_weight[0], offset, total) for offset in (-1, 0, 1)]
    south = [cycle_interp(south_rows, cycle_shift[1], cycle_weight[1], offset, total) for offset in (-1, 0, 1)]
    center = [jnp.roll(field, -offset, axis=1) for offset in (-1, 0, 1)]
    metric = cycle_scale[:, None]
    alpha_t = 0.5 * (south[1] - north[1])
    alpha_p = 0.5 * metric * (center[2] - center[0])
    shear_tt = south[1] - 2.0 * center[1] + north[1]
    shear_pp = metric * metric * (center[2] - 2.0 * center[1] + center[0])
    shear_tp = 0.25 * metric * (south[2] - south[0] - north[2] + north[0])
    return alpha_t, alpha_p, shear_tt, shear_pp, shear_tp


def advance(state, fields, gain):
    disp_t, disp_p, a_zz, a_zo, a_oz, a_oo = state
    alpha_t, alpha_p, shear_tt, shear_pp, shear_tp = fields
    new_t = disp_t - gain * (alpha_t + shear_tt * disp_t + shear_tp * disp_p)
    new_p = disp_p - gain * (alpha_p + shear_tp * disp_t + shear_pp * disp_p)
    b_zz = a_zz - gain * (shear_tt * a_zz + shear_tp * a_oz)
    b_zo = a_zo - gain * (shear_tt * a_zo + shear_tp * a_oo)
    b_oz = a_oz - gain * (shear_tp * a_zz + shear_pp * a_oz)
    b_oo = a_oo - gain * (shear_tp * a_zo + shear_pp * a_oo)
    return (new_t, new_p, b_zz, b_zo, b_oz, b_oo)


def reference(potential, lens_weight, cycle_shift, cycle_weight, cycle_scale):
    turn = NLON // 4
    skies = [jnp.roll(potential[plane_k], -turn, axis=1) for plane_k in range(PLANES)]

    def one_source(gains):
        zeros = jnp.zeros((ROWS, NLON), jnp.float32)
        ones = jnp.ones((ROWS, NLON), jnp.float32)
        state = (zeros, zeros, ones, zeros, zeros, ones)
        for plane_k in range(PLANES):
            fields = derivatives(skies[plane_k], cycle_shift, cycle_weight, cycle_scale)
            state = advance(state, fields, gains[plane_k])
        return jnp.stack(state)

    result = lax.map(one_source, lens_weight)
    return result[:, 0:2], result[:, 2:6]
```

```python
import jax
import jax.numpy as jnp
from jax import lax
from jax.experimental import pallas as pl
from jax.experimental.pallas import tpu as pltpu
from jax.sharding import PartitionSpec as P

HALO = 4
TAPS = 7
PAD = 16
Z_LO, Z_HI, NX, RING = 4, 2, 4, 16


def z_move(value, ahead, steps=0):
    pairs = []
    for z_lo in range(Z_LO):
        for z_hi in range(Z_HI):
            for ring in range(RING):
                for x in range(NX):
                    z = (z_hi * Z_LO + z_lo + ahead) % (Z_LO * Z_HI)
                    lon = (((z_lo + 1) % Z_LO) * RING + ring + steps) % (Z_LO * RING)
                    source = lon * Z_HI * NX + (z // Z_LO) * NX + x
                    target = (z_lo * RING + ring) * Z_HI * NX + z_hi * NX + x
                    pairs.append((source, target))
    return lax.ppermute(value, ("lon", "plane"), pairs)


def x_move(value, ahead):
    pairs = [
        (z_hi * NX + (x + ahead) % NX, z_hi * NX + x) for z_hi in range(Z_HI) for x in range(NX)
    ]
    return lax.ppermute(value, "plane", pairs)


def load_planes(slot_ref, tiles, ext):
    for ahead, tile in enumerate(tiles):
        slot = slot_ref[ahead]
        width = tile.shape[1]
        for half in range(2):
            rows = slice(half * 128, half * 128 + 128)
            ext[slot, half, PAD : PAD + width, :] = tile[rows, :].T
            ext[slot, half, PAD - HALO : PAD, :] = tile[width : width + HALO, rows]
            ext[slot, half, PAD + width : PAD + width + HALO, :] = tile[
                width + HALO : width + 2 * HALO, rows
            ]


def neighbours(width, taps_ref, ext, diff, both):
    lane = lax.broadcasted_iota(jnp.int32, (8, 128), 1)
    first, last = lane == 0, lane == 127

    def block(j, carry):
        at = pl.multiple_of(j * 8, 8) + PAD - 8
        norths, souths = [], []
        for half in range(2):
            north_of, south_of = [], []
            for slot in range(NX):
                views = [ext[slot, half, pl.ds(at + tap - 3, 8), :] for tap in range(TAPS)]
                north = views[0] * taps_ref[0, half]
                south = views[0] * taps_ref[TAPS, half]
                for tap in range(1, TAPS):
                    north += views[tap] * taps_ref[tap, half]
                    south += views[tap] * taps_ref[TAPS + tap, half]
                north_of.append(pltpu.roll(north, 1, 1))
                south_of.append(pltpu.roll(south, 127, 1))
            norths.append(north_of)
            souths.append(south_of)
        for slot in range(NX):
            n = [
                jnp.where(first, 0.0, norths[0][slot]),
                jnp.where(first, norths[0][slot], norths[1][slot]),
            ]
            s = [
                jnp.where(last, souths[1][slot], souths[0][slot]),
                jnp.where(last, 0.0, souths[1][slot]),
            ]
            for half in range(2):
                diff[slot, half, pl.ds(at, 8), :] = s[half] - n[half]
                both[slot, half, pl.ds(at, 8), :] = s[half] + n[half]
        return carry

    lax.fori_loop(0, width // 8 + 2, block, 0)


def compose(at, half, hi, gain_ref, metric_ref, ext, diff, both):
    half_m, square_m, quarter_m = metric_ref[0, half], metric_ref[1, half], metric_ref[2, half]
    state = None
    for slot in range(NX):
        gain = gain_ref[hi * NX + slot]
        centre = ext[slot, half, pl.ds(at, 8), :]
        east = ext[slot, half, pl.ds(at + 1, 8), :]
        west = ext[slot, half, pl.ds(at - 1, 8), :]
        twice = centre + centre
        alpha_t = (0.5 * gain) * diff[slot, half, pl.ds(at, 8), :]
        alpha_p = (gain * half_m) * (east - west)
        u_tt = gain * (both[slot, half, pl.ds(at, 8), :] - twice)
        u_pp = (gain * square_m) * ((east + west) - twice)
        u_tp = (gain * quarter_m) * (
            diff[slot, half, pl.ds(at + 1, 8), :] - diff[slot, half, pl.ds(at - 1, 8), :]
        )
        if state is None:
            state = (-alpha_t, -alpha_p, 1.0 - u_tt, -u_tp, -u_tp, 1.0 - u_pp)
        else:
            d_t, d_p, a_zz, a_zo, a_oz, a_oo = state
            state = (
                d_t - (alpha_t + (u_tt * d_t + u_tp * d_p)),
                d_p - (alpha_p + (u_tp * d_t + u_pp * d_p)),
                a_zz - (u_tt * a_zz + u_tp * a_oz),
                a_zo - (u_tt * a_zo + u_tp * a_oo),
                a_oz - (u_tp * a_zz + u_pp * a_oz),
                a_oo - (u_tp * a_zo + u_pp * a_oo),
            )
    return state


def first_kernel(slot_ref, gain_ref, taps_ref, metric_ref, t0, t1, t2, t3, out, ext, diff, both):
    width = t0.shape[1]
    load_planes(slot_ref, (t0, t1, t2, t3), ext)
    neighbours(width, taps_ref, ext, diff, both)
    hi = slot_ref[NX]

    def block(j, carry):
        at = pl.multiple_of(j * 8, 8)
        for half in range(2):
            state = compose(at + PAD, half, hi, gain_ref, metric_ref, ext, diff, both)
            for k in range(6):
                out[k, half, pl.ds(at, 8), :] = state[k]
        return carry

    lax.fori_loop(0, width // 8, block, 0)


def second_kernel(
    slot_ref, gain_ref, taps_ref, metric_ref, t0, t1, t2, t3, other, disp, jac, ext, diff, both, done
):
    width = t0.shape[1]
    load_planes(slot_ref, (t0, t1, t2, t3), ext)
    neighbours(width, taps_ref, ext, diff, both)
    hi = 1 - slot_ref[NX]
    other_first = hi == 1

    def block(j, carry):
        at = pl.multiple_of(j * 8, 8)
        for half in range(2):
            here = compose(at + PAD, half, hi, gain_ref, metric_ref, ext, diff, both)
            there = [other[k, half, pl.ds(at, 8), :] for k in range(6)]
            d_t, d_p, a_zz, a_zo, a_oz, a_oo = [
                jnp.where(other_first, a, b) for a, b in zip(there, here)
            ]
            e_t, e_p, b_zz, b_zo, b_oz, b_oo = [
                jnp.where(other_first, b, a) for a, b in zip(there, here)
            ]
            state = (
                e_t + (b_zz * d_t + b_zo * d_p),
                e_p + (b_oz * d_t + b_oo * d_p),
                b_zz * a_zz + b_zo * a_oz,
                b_zz * a_zo + b_zo * a_oo,
                b_oz * a_zz + b_oo * a_oz,
                b_oz * a_zo + b_oo * a_oo,
            )
            for k in range(6):
                done[k, half, pl.ds(at, 8), :] = state[k]
        return carry

    lax.fori_loop(0, width // 8, block, 0)
    for k in range(6):
        for half in range(2):
            rows = slice(half * 128, half * 128 + 128)
            turned = done[k, half].T
            if k < 2:
                disp[k, rows, :] = turned
            else:
                jac[k - 2, rows, :] = turned


def smem():
    return pl.BlockSpec(memory_space=pltpu.SMEM)


def vmem():
    return pl.BlockSpec(memory_space=pltpu.VMEM)


def planes_scratch(width):
    return [pltpu.VMEM((NX, 2, width + 2 * PAD, 128), jnp.float32)] * 3


def cost(rows, width):
    return pl.CostEstimate(
        flops=260 * NX * rows * width, bytes_accessed=40 * rows * width, transcendentals=0
    )


def prepare_kernel(tile_ref, shift_ref, weight_ref, scale_ref, low, high, taps, metric):
    rows, width = tile_ref.shape
    for half in range(2):
        lanes = slice(half * 128, half * 128 + 128)
        low[:, lanes] = tile_ref[lanes, width - 128 :].T[128 - HALO :]
        high[:, lanes] = tile_ref[lanes, :128].T[:HALO]
    for side, turn in ((0, rows - 1), (1, 1)):
        shift = jnp.broadcast_to(shift_ref[side : side + 1, :], (8, rows))
        frac = jnp.broadcast_to(weight_ref[side : side + 1, :].astype(jnp.float32) / 16.0, (8, rows))
        shift, frac = pltpu.roll(shift, turn, 1), pltpu.roll(frac, turn, 1)
        for tap in range(TAPS):
            value = jnp.where(shift == tap - 3, 1.0 - frac, 0.0)
            value += jnp.where(shift == tap - 4, frac, 0.0)
            for half in range(2):
                taps[side * TAPS + tap, half] = value[:, half * 128 : half * 128 + 128]
    scale = jnp.broadcast_to(scale_ref[...], (8, rows))
    for k, value in enumerate((0.5 * scale, scale * scale, 0.25 * scale)):
        for half in range(2):
            metric[k, half] = value[:, half * 128 : half * 128 + 128]


def prepare(tile, cycle_shift, cycle_weight, cycle_scale):
    rows = tile.shape[0]
    return pl.pallas_call(
        prepare_kernel,
        out_shape=(
            jax.ShapeDtypeStruct((HALO, rows), jnp.float32),
            jax.ShapeDtypeStruct((HALO, rows), jnp.float32),
            jax.ShapeDtypeStruct((2 * TAPS, 2, 8, rows // 2), jnp.float32),
            jax.ShapeDtypeStruct((3, 2, 8, rows // 2), jnp.float32),
        ),
        in_specs=[vmem()] * 4,
        out_specs=(vmem(),) * 4,
        cost_estimate=pl.CostEstimate(flops=1 << 16, bytes_accessed=1 << 20, transcendentals=0),
        name="prepare",
    )(tile, cycle_shift, cycle_weight, cycle_scale[None])


def per_device(potential, lens_weight, cycle_shift, cycle_weight, cycle_scale):
    tile = potential[0]
    rows, width = tile.shape
    gains = lens_weight[0]
    lon, plane = lax.axis_index("lon"), lax.axis_index("plane")
    x = plane % NX
    near_hi = (((plane // NX) * Z_LO + lon // RING + 1) // Z_LO) % Z_HI
    order = jnp.arange(2 * NX, dtype=jnp.int32)
    scalars = jnp.where(order < NX, (x + order) % NX, near_hi).astype(jnp.int32)

    near = z_move(tile, 1)
    far = z_move(tile, 1 + Z_LO)
    low, high, taps, metric = prepare(tile, cycle_shift, cycle_weight, cycle_scale)

    def group(own, low, high, ahead):
        whole = jnp.concatenate([own, z_move(low, ahead, -1), z_move(high, ahead, 1)])
        return (whole, x_move(whole, 1), x_move(whole, 2), x_move(whole, 3))

    near_tiles = group(near, low, high, 1)
    low, high, _ = lax.optimization_barrier((low, high, near_tiles[0]))
    far_tiles = group(far, low, high, 1 + Z_LO)

    state = pl.pallas_call(
        first_kernel,
        out_shape=jax.ShapeDtypeStruct((6, 2, width, rows // 2), jnp.float32),
        in_specs=[smem(), smem()] + [vmem()] * 6,
        out_specs=vmem(),
        scratch_shapes=planes_scratch(width),
        cost_estimate=cost(rows, width),
        compiler_params=pltpu.CompilerParams(vmem_limit_bytes=24 << 20),
        name="near_planes",
    )(scalars, gains, taps, metric, *near_tiles)
    displacement, jacobian = pl.pallas_call(
        second_kernel,
        out_shape=(
            jax.ShapeDtypeStruct((2, rows, width), jnp.float32),
            jax.ShapeDtypeStruct((4, rows, width), jnp.float32),
        ),
        in_specs=[smem(), smem()] + [vmem()] * 7,
        out_specs=(vmem(), vmem()),
        scratch_shapes=planes_scratch(width)
        + [pltpu.VMEM((6, 2, width, rows // 2), jnp.float32)],
        cost_estimate=cost(rows, width),
        compiler_params=pltpu.CompilerParams(vmem_limit_bytes=24 << 20),
        name="far_planes",
    )(scalars, gains, taps, metric, *far_tiles, state)
    return displacement[None], jacobian[None]


def solution(mesh):
    in_specs = (P("plane", None, "lon"), P("plane", None), P(), P(), P())
    out_specs = (P("plane", None, None, "lon"), P("plane", None, None, "lon"))
    return jax.shard_map(
        per_device, mesh=mesh, in_specs=in_specs, out_specs=out_specs, check_vma=False
    )
```

```python
import jax
import jax.numpy as jnp
from jax import lax
from jax.experimental import pallas as pl
from jax.experimental.pallas import tpu as pltpu
from jax.sharding import PartitionSpec as P

HALO = 4
TAPS = 7
PAD = 24
STEP = 48
BLOCK = 16
AHEAD = (0, 1, 3, 2)
Z_LO, Z_HI, NX, RING = 4, 2, 4, 16


def z_move(value, ahead, steps=0):
    pairs = []
    for z_lo in range(Z_LO):
        for z_hi in range(Z_HI):
            for ring in range(RING):
                for x in range(NX):
                    z = (z_hi * Z_LO + z_lo + ahead) % (Z_LO * Z_HI)
                    lon = (((z_lo + 1) % Z_LO) * RING + ring + steps) % (Z_LO * RING)
                    source = lon * Z_HI * NX + (z // Z_LO) * NX + x
                    target = (z_lo * RING + ring) * Z_HI * NX + z_hi * NX + x
                    pairs.append((source, target))
    return lax.ppermute(value, ("lon", "plane"), pairs)


def swap(value):
    pairs = [(z_hi * NX + x, (1 - z_hi) * NX + x) for z_hi in range(Z_HI) for x in range(NX)]
    return lax.ppermute(value, "plane", pairs)


def x_move(value, ahead):
    pairs = [
        (z_hi * NX + (x + ahead) % NX, z_hi * NX + x) for z_hi in range(Z_HI) for x in range(NX)
    ]
    return lax.ppermute(value, "plane", pairs)


def load_planes(slot_ref, tiles, ext):
    for ahead, tile in zip(AHEAD, tiles):
        slot = slot_ref[ahead].astype(jnp.int32)
        width = tile.shape[1]
        for half in range(2):
            rows = slice(half * 128, half * 128 + 128)
            ext[slot, half, PAD : PAD + width, :] = tile[rows, :].T
            ext[slot, half, PAD - HALO : PAD, :] = tile[width : width + HALO, rows]
            ext[slot, half, PAD + width : PAD + width + HALO, :] = tile[
                width + HALO : width + 2 * HALO, rows
            ]


def stencils(width, taps_ref, ext, fields):
    lane = lax.broadcasted_iota(jnp.int32, (STEP // 8, 8, 128), 2)
    first, last = lane == 0, lane == 127
    start = PAD - 16

    def step(i, carry):
        at = pl.multiple_of(start + i * STEP, 8)
        for slot in range(NX):
            norths, souths, centres = [], [], []
            for half in range(2):
                views = [
                    ext[slot, half, pl.ds(at + tap - 3, STEP), :].reshape(STEP // 8, 8, 128)
                    for tap in range(TAPS)
                ]
                north = views[0] * taps_ref[0, half]
                south = views[0] * taps_ref[TAPS, half]
                for tap in range(1, TAPS):
                    north += views[tap] * taps_ref[tap, half]
                    south += views[tap] * taps_ref[TAPS + tap, half]
                twice = views[3] + views[3]
                east, west = views[4], views[2]
                fields[slot, half, 2, pl.ds(at, STEP), :] = (east - west).reshape(STEP, 128)
                fields[slot, half, 3, pl.ds(at, STEP), :] = (east + west - twice).reshape(STEP, 128)
                norths.append(pltpu.roll(north.reshape(STEP, 128), 1, 1).reshape(north.shape))
                souths.append(pltpu.roll(south.reshape(STEP, 128), 127, 1).reshape(north.shape))
                centres.append(twice)
            n = [jnp.where(first, 0.0, norths[0]), jnp.where(first, norths[0], norths[1])]
            s = [jnp.where(last, souths[1], souths[0]), jnp.where(last, 0.0, souths[1])]
            for half in range(2):
                fields[slot, half, 0, pl.ds(at, STEP), :] = (s[half] - n[half]).reshape(STEP, 128)
                fields[slot, half, 1, pl.ds(at, STEP), :] = (
                    s[half] + n[half] - centres[half]
                ).reshape(STEP, 128)
        return carry

    lax.fori_loop(0, (width + 2 * 16) // STEP, step, 0)


def compose(at, half, hi, scalar_ref, metric_ref, fields):
    half_m, square_m, quarter_m = metric_ref[0, half], metric_ref[1, half], metric_ref[2, half]

    def load(slot, k, shift=0):
        return fields[slot, half, k, pl.ds(at + shift, BLOCK), :].reshape(BLOCK // 8, 8, 128)

    state = None
    for slot in range(NX):
        gain = scalar_ref[NX + 1 + hi * NX + slot]
        alpha_t = (0.5 * gain) * load(slot, 0)
        alpha_p = (gain * half_m) * load(slot, 2)
        u_tt = gain * load(slot, 1)
        u_pp = (gain * square_m) * load(slot, 3)
        u_tp = (gain * quarter_m) * (load(slot, 0, 1) - load(slot, 0, -1))
        if state is None:
            state = (-alpha_t, -alpha_p, 1.0 - u_tt, -u_tp, -u_tp, 1.0 - u_pp)
        else:
            d_t, d_p, a_zz, a_zo, a_oz, a_oo = state
            state = (
                d_t - (alpha_t + (u_tt * d_t + u_tp * d_p)),
                d_p - (alpha_p + (u_tp * d_t + u_pp * d_p)),
                a_zz - (u_tt * a_zz + u_tp * a_oz),
                a_zo - (u_tt * a_zo + u_tp * a_oo),
                a_oz - (u_tp * a_zz + u_pp * a_oz),
                a_oo - (u_tp * a_zo + u_pp * a_oo),
            )
    return state


def begin(scalar_ref, taps_hbm, metric_hbm, tiles, ext, fields, taps, metric, sems):
    copies = [
        pltpu.make_async_copy(taps_hbm, taps, sems.at[0]),
        pltpu.make_async_copy(metric_hbm, metric, sems.at[1]),
    ]
    for copy in copies:
        copy.start()
    load_planes(scalar_ref, tiles, ext)
    for copy in copies:
        copy.wait()
    stencils(tiles[0].shape[1], taps, ext, fields)


def first_kernel(
    scalar_ref, taps_hbm, metric_hbm, t0, t1, t2, t3, out, ext, fields, taps, metric, sems
):
    begin(scalar_ref, taps_hbm, metric_hbm, (t0, t1, t2, t3), ext, fields, taps, metric, sems)
    hi = scalar_ref[NX].astype(jnp.int32)

    def block(j, carry):
        at = pl.multiple_of(j * BLOCK, BLOCK)
        for half in range(2):
            state = compose(at + PAD, half, hi, scalar_ref, metric, fields)
            for k in range(6):
                out[k, half, pl.ds(at, BLOCK), :] = state[k].reshape(BLOCK, 128)
        return carry

    lax.fori_loop(0, t0.shape[1] // BLOCK, block, 0)


def second_kernel(
    scalar_ref,
    taps_hbm,
    metric_hbm,
    t0,
    t1,
    t2,
    t3,
    other,
    disp,
    jac,
    ext,
    fields,
    taps,
    metric,
    sems,
    done,
):
    begin(scalar_ref, taps_hbm, metric_hbm, (t0, t1, t2, t3), ext, fields, taps, metric, sems)
    hi = 1 - scalar_ref[NX].astype(jnp.int32)
    other_first = hi == 1

    def block(j, carry):
        at = pl.multiple_of(j * BLOCK, BLOCK)
        for half in range(2):
            here = compose(at + PAD, half, hi, scalar_ref, metric, fields)
            there = [
                other[k, half, pl.ds(at, BLOCK), :].reshape(BLOCK // 8, 8, 128) for k in range(6)
            ]
            d_t, d_p, a_zz, a_zo, a_oz, a_oo = [
                jnp.where(other_first, a, b) for a, b in zip(there, here)
            ]
            e_t, e_p, b_zz, b_zo, b_oz, b_oo = [
                jnp.where(other_first, b, a) for a, b in zip(there, here)
            ]
            state = (
                e_t + (b_zz * d_t + b_zo * d_p),
                e_p + (b_oz * d_t + b_oo * d_p),
                b_zz * a_zz + b_zo * a_oz,
                b_zz * a_zo + b_zo * a_oo,
                b_oz * a_zz + b_oo * a_oz,
                b_oz * a_zo + b_oo * a_oo,
            )
            for k in range(6):
                done[k, half, pl.ds(at, BLOCK), :] = state[k].reshape(BLOCK, 128)
        return carry

    lax.fori_loop(0, t0.shape[1] // BLOCK, block, 0)
    for k in range(6):
        for half in range(2):
            rows = slice(half * 128, half * 128 + 128)
            turned = done[k, half].T
            if k < 2:
                disp[k, rows, :] = turned
            else:
                jac[k - 2, rows, :] = turned


def smem():
    return pl.BlockSpec(memory_space=pltpu.SMEM)


def vmem():
    return pl.BlockSpec(memory_space=pltpu.VMEM)


def scratch(rows, width):
    return [
        pltpu.VMEM((NX, 2, width + 2 * PAD, rows // 2), jnp.float32),
        pltpu.VMEM((NX, 2, 4, width + 2 * PAD, rows // 2), jnp.float32),
        pltpu.VMEM((2 * TAPS, 2, 8, rows // 2), jnp.float32),
        pltpu.VMEM((3, 2, 8, rows // 2), jnp.float32),
        pltpu.SemaphoreType.DMA((2,)),
    ]


def cost(rows, width):
    return pl.CostEstimate(
        flops=260 * NX * rows * width, bytes_accessed=40 * rows * width, transcendentals=0
    )


def prepare_kernel(tile_ref, shift_ref, weight_ref, scale_ref, low, high, taps, metric):
    rows, width = tile_ref.shape
    for half in range(2):
        lanes = slice(half * 128, half * 128 + 128)
        low[:, lanes] = tile_ref[lanes, width - 128 :].T[128 - HALO :]
        high[:, lanes] = tile_ref[lanes, :128].T[:HALO]
    for side, turn in ((0, rows - 1), (1, 1)):
        shift = jnp.broadcast_to(shift_ref[side : side + 1, :], (8, rows))
        frac = jnp.broadcast_to(weight_ref[side : side + 1, :].astype(jnp.float32) / 16.0, (8, rows))
        shift, frac = pltpu.roll(shift, turn, 1), pltpu.roll(frac, turn, 1)
        for tap in range(TAPS):
            value = jnp.where(shift == tap - 3, 1.0 - frac, 0.0)
            value += jnp.where(shift == tap - 4, frac, 0.0)
            for half in range(2):
                taps[side * TAPS + tap, half] = value[:, half * 128 : half * 128 + 128]
    scale = jnp.broadcast_to(scale_ref[...], (8, rows))
    for k, value in enumerate((0.5 * scale, scale * scale, 0.25 * scale)):
        for half in range(2):
            metric[k, half] = value[:, half * 128 : half * 128 + 128]


def prepare(tile, cycle_shift, cycle_weight, cycle_scale):
    rows = tile.shape[0]
    return pl.pallas_call(
        prepare_kernel,
        out_shape=(
            jax.ShapeDtypeStruct((HALO, rows), jnp.float32),
            jax.ShapeDtypeStruct((HALO, rows), jnp.float32),
            jax.ShapeDtypeStruct((2 * TAPS, 2, 8, rows // 2), jnp.float32),
            jax.ShapeDtypeStruct((3, 2, 8, rows // 2), jnp.float32),
        ),
        in_specs=[vmem()] * 4,
        out_specs=(vmem(),) * 4,
        cost_estimate=pl.CostEstimate(flops=1 << 16, bytes_accessed=1 << 20, transcendentals=0),
        name="prepare",
    )(tile, cycle_shift, cycle_weight, cycle_scale[None])


def per_device(potential, lens_weight, cycle_shift, cycle_weight, cycle_scale):
    tile = potential[0]
    rows, width = tile.shape
    lon, plane = lax.axis_index("lon"), lax.axis_index("plane")
    x = plane % NX
    near_hi = (((plane // NX) * Z_LO + lon // RING + 1) // Z_LO) % Z_HI
    order = jnp.arange(NX + 1, dtype=jnp.int32)
    places = jnp.where(order < NX, (x + order) % NX, near_hi).astype(jnp.float32)
    scalars = jnp.concatenate([places, lens_weight[0]])

    low, high, taps, metric = prepare(tile, cycle_shift, cycle_weight, cycle_scale)
    near, far = z_move(tile, 1), z_move(tile, 1 + Z_LO)
    strips = jnp.concatenate([z_move(low, 1, -1), z_move(high, 1, 1)])
    near = jnp.concatenate([near, strips])
    near_tiles = tuple([near] + [x_move(near, ahead) for ahead in AHEAD[1:]])
    far = jnp.concatenate([far, swap(strips)])
    far_tiles = tuple([far] + [x_move(far, ahead) for ahead in AHEAD[1:]])

    in_hbm = pl.BlockSpec(memory_space=pltpu.HBM)
    state = pl.pallas_call(
        first_kernel,
        out_shape=jax.ShapeDtypeStruct((6, 2, width, rows // 2), jnp.float32),
        in_specs=[smem(), in_hbm, in_hbm] + [vmem()] * 4,
        out_specs=vmem(),
        scratch_shapes=scratch(rows, width),
        cost_estimate=cost(rows, width),
        compiler_params=pltpu.CompilerParams(vmem_limit_bytes=24 << 20),
        name="near_planes",
    )(scalars, taps, metric, *near_tiles)
    displacement, jacobian = pl.pallas_call(
        second_kernel,
        out_shape=(
            jax.ShapeDtypeStruct((2, rows, width), jnp.float32),
            jax.ShapeDtypeStruct((4, rows, width), jnp.float32),
        ),
        in_specs=[smem(), in_hbm, in_hbm] + [vmem()] * 5,
        out_specs=(vmem(), vmem()),
        scratch_shapes=scratch(rows, width)
        + [pltpu.VMEM((6, 2, width, rows // 2), jnp.float32)],
        cost_estimate=cost(rows, width),
        compiler_params=pltpu.CompilerParams(vmem_limit_bytes=24 << 20),
        name="far_planes",
    )(scalars, taps, metric, *far_tiles, state)
    return displacement[None], jacobian[None]


def solution(mesh):
    in_specs = (P("plane", None, "lon"), P("plane", None), P(), P(), P())
    out_specs = (P("plane", None, None, "lon"), P("plane", None, None, "lon"))
    return jax.shard_map(
        per_device, mesh=mesh, in_specs=in_specs, out_specs=out_specs, check_vma=False
    )
```

```python
import jax
import jax.numpy as jnp
from jax import lax
from jax.experimental import pallas as pl
from jax.experimental.pallas import tpu as pltpu
from jax.sharding import PartitionSpec as P

HALO = 4
TAPS = 7
PAD = 24
STEP = 48
BLOCK = 16
NEAR = (0, 1, 3, 2)
FAR = (0, 3, 2, 1)
Z_LO, Z_HI, NX, RING = 4, 2, 4, 16


def z_move(value, ahead, steps=0):
    pairs = []
    for z_lo in range(Z_LO):
        for z_hi in range(Z_HI):
            for ring in range(RING):
                for x in range(NX):
                    z = (z_hi * Z_LO + z_lo + ahead) % (Z_LO * Z_HI)
                    lon = (((z_lo + 1) % Z_LO) * RING + ring + steps) % (Z_LO * RING)
                    source = lon * Z_HI * NX + (z // Z_LO) * NX + x
                    target = (z_lo * RING + ring) * Z_HI * NX + z_hi * NX + x
                    pairs.append((source, target))
    return lax.ppermute(value, ("lon", "plane"), pairs)


def swap(value):
    pairs = [(z_hi * NX + x, (1 - z_hi) * NX + x) for z_hi in range(Z_HI) for x in range(NX)]
    return lax.ppermute(value, "plane", pairs)


def x_move(value, ahead):
    pairs = [
        (z_hi * NX + (x + ahead) % NX, z_hi * NX + x) for z_hi in range(Z_HI) for x in range(NX)
    ]
    return lax.ppermute(value, "plane", pairs)


def load_planes(slots, tiles, ext):
    for slot, tile in zip(slots, tiles):
        width = tile.shape[1]
        for half in range(2):
            rows = slice(half * 128, half * 128 + 128)
            ext[slot, half, PAD : PAD + width, :] = tile[rows, :].T
            ext[slot, half, PAD - HALO : PAD, :] = tile[width : width + HALO, rows]
            ext[slot, half, PAD + width : PAD + width + HALO, :] = tile[
                width + HALO : width + 2 * HALO, rows
            ]


def stencils(width, taps_ref, ext, fields):
    lane = lax.broadcasted_iota(jnp.int32, (STEP // 8, 8, 128), 2)
    first, last = lane == 0, lane == 127
    start = PAD - 16

    def step(i, carry):
        at = pl.multiple_of(start + i * STEP, 8)
        for slot in range(ext.shape[0]):
            norths, souths, centres = [], [], []
            for half in range(2):
                views = [
                    ext[slot, half, pl.ds(at + tap - 3, STEP), :].reshape(STEP // 8, 8, 128)
                    for tap in range(TAPS)
                ]
                north = views[0] * taps_ref[0, half]
                south = views[0] * taps_ref[TAPS, half]
                for tap in range(1, TAPS):
                    north += views[tap] * taps_ref[tap, half]
                    south += views[tap] * taps_ref[TAPS + tap, half]
                twice = views[3] + views[3]
                east, west = views[4], views[2]
                fields[slot, half, 2, pl.ds(at, STEP), :] = (east - west).reshape(STEP, 128)
                fields[slot, half, 3, pl.ds(at, STEP), :] = (east + west - twice).reshape(STEP, 128)
                norths.append(pltpu.roll(north.reshape(STEP, 128), 1, 1).reshape(north.shape))
                souths.append(pltpu.roll(south.reshape(STEP, 128), 127, 1).reshape(north.shape))
                centres.append(twice)
            n = [jnp.where(first, 0.0, norths[0]), jnp.where(first, norths[0], norths[1])]
            s = [jnp.where(last, souths[1], souths[0]), jnp.where(last, 0.0, souths[1])]
            for half in range(2):
                fields[slot, half, 0, pl.ds(at, STEP), :] = (s[half] - n[half]).reshape(STEP, 128)
                fields[slot, half, 1, pl.ds(at, STEP), :] = (
                    s[half] + n[half] - centres[half]
                ).reshape(STEP, 128)
        return carry

    lax.fori_loop(0, (width + 2 * 16) // STEP, step, 0)


def compose(half, hi, tables, load):
    half_m, square_m, quarter_m = [tables[2 * TAPS + k, half] for k in range(3)]
    state = None
    for slot in range(NX):
        gain = tables[2 * TAPS + 3 + hi * (NX // 2) + slot // 2, slot % 2]
        alpha_t = (0.5 * gain) * load(slot, 0)
        alpha_p = (gain * half_m) * load(slot, 2)
        u_tt = gain * load(slot, 1)
        u_pp = (gain * square_m) * load(slot, 3)
        u_tp = (gain * quarter_m) * (load(slot, 0, 1) - load(slot, 0, -1))
        if state is None:
            state = (-alpha_t, -alpha_p, 1.0 - u_tt, -u_tp, -u_tp, 1.0 - u_pp)
        else:
            d_t, d_p, a_zz, a_zo, a_oz, a_oo = state
            state = (
                d_t - (alpha_t + (u_tt * d_t + u_tp * d_p)),
                d_p - (alpha_p + (u_tp * d_t + u_pp * d_p)),
                a_zz - (u_tt * a_zz + u_tp * a_oz),
                a_zo - (u_tt * a_zo + u_tp * a_oo),
                a_oz - (u_tp * a_zz + u_pp * a_oz),
                a_oo - (u_tp * a_zo + u_pp * a_oo),
            )
    return state


def block_of(ref, at):
    return ref[pl.ds(at, BLOCK), :].reshape(BLOCK // 8, 8, 128)


def near_kernel(scalar_ref, tables, t0, t1, t2, t3, out, ext, fields):
    width = t0.shape[1]
    slots = [lax.rem(scalar_ref[0] + ahead, NX) for ahead in NEAR]
    load_planes(slots, (t0, t1, t2, t3), ext)
    stencils(width, tables, ext, fields)
    hi = scalar_ref[1]

    def block(j, carry):
        at = pl.multiple_of(j * BLOCK, BLOCK)
        for half in range(2):

            def load(slot, k, shift=0):
                return block_of(fields.at[slot, half, k], at + PAD + shift)

            state = compose(half, hi, tables, load)
            for k in range(6):
                out[k, half, pl.ds(at, BLOCK), :] = state[k].reshape(BLOCK, 128)
        return carry

    lax.fori_loop(0, width // BLOCK, block, 0)


def early_kernel(tables, t0, t1, t2, after, fields, ext):
    load_planes(range(3), (t0, t1, t2), ext)
    stencils(t0.shape[1], tables, ext, fields)


def far_kernel(scalar_ref, tables, last, early, other, disp, jac, ext, fields, done):
    width = last.shape[1]
    load_planes(range(1), (last,), ext)
    stencils(width, tables, ext, fields)
    hi = 1 - scalar_ref[1]
    other_first = hi == 1

    def rays(x):
        def block(j, carry):
            at = pl.multiple_of(j * BLOCK, BLOCK)
            for half in range(2):

                def load(slot, k, shift=0):
                    tile = FAR.index((slot - x) % NX)
                    ref = fields.at[0] if tile == NX - 1 else early.at[tile]
                    return block_of(ref.at[half, k], at + PAD + shift)

                here = compose(half, hi, tables, load)
                there = [block_of(other.at[k, half], at) for k in range(6)]
                d_t, d_p, a_zz, a_zo, a_oz, a_oo = [
                    jnp.where(other_first, a, b) for a, b in zip(there, here)
                ]
                e_t, e_p, b_zz, b_zo, b_oz, b_oo = [
                    jnp.where(other_first, b, a) for a, b in zip(there, here)
                ]
                state = (
                    e_t + (b_zz * d_t + b_zo * d_p),
                    e_p + (b_oz * d_t + b_oo * d_p),
                    b_zz * a_zz + b_zo * a_oz,
                    b_zz * a_zo + b_zo * a_oo,
                    b_oz * a_zz + b_oo * a_oz,
                    b_oz * a_zo + b_oo * a_oo,
                )
                for k in range(6):
                    done[k, half, pl.ds(at, BLOCK), :] = state[k].reshape(BLOCK, 128)
            return carry

        lax.fori_loop(0, width // BLOCK, block, 0)

    for x in range(NX):
        pl.when(scalar_ref[0] == x)(lambda x=x: rays(x))
    for k in range(6):
        for half in range(2):
            rows = slice(half * 128, half * 128 + 128)
            turned = done[k, half].T
            if k < 2:
                disp[k, rows, :] = turned
            else:
                jac[k - 2, rows, :] = turned


def smem():
    return pl.BlockSpec(memory_space=pltpu.SMEM)


def vmem():
    return pl.BlockSpec(memory_space=pltpu.VMEM)


def ext_shape(count, rows, width):
    return (count, 2, width + 2 * PAD, rows // 2)


def fields_shape(count, rows, width):
    return (count, 2, 4, width + 2 * PAD, rows // 2)


def cost(planes, rows, width):
    return pl.CostEstimate(
        flops=260 * planes * rows * width, bytes_accessed=40 * rows * width, transcendentals=0
    )


def prepare_kernel(tile_ref, shift_ref, weight_ref, scale_ref, gain_ref, low, high, tables):
    rows, width = tile_ref.shape
    for half in range(2):
        lanes = slice(half * 128, half * 128 + 128)
        low[:, lanes] = tile_ref[lanes, width - 128 :].T[128 - HALO :]
        high[:, lanes] = tile_ref[lanes, :128].T[:HALO]
    for side, turn in ((0, rows - 1), (1, 1)):
        shift = jnp.broadcast_to(shift_ref[side : side + 1, :], (8, rows))
        frac = jnp.broadcast_to(weight_ref[side : side + 1, :].astype(jnp.float32) / 16.0, (8, rows))
        shift, frac = pltpu.roll(shift, turn, 1), pltpu.roll(frac, turn, 1)
        for tap in range(TAPS):
            value = jnp.where(shift == tap - 3, 1.0 - frac, 0.0)
            value += jnp.where(shift == tap - 4, frac, 0.0)
            for half in range(2):
                tables[side * TAPS + tap, half] = value[:, half * 128 : half * 128 + 128]
    scale = jnp.broadcast_to(scale_ref[...], (8, rows))
    for k, value in enumerate((0.5 * scale, scale * scale, 0.25 * scale)):
        for half in range(2):
            tables[2 * TAPS + k, half] = value[:, half * 128 : half * 128 + 128]
    for k in range(gain_ref.shape[1]):
        tables[2 * TAPS + 3 + k // 2, k % 2] = jnp.broadcast_to(gain_ref[:, k : k + 1], (8, rows // 2))


def prepare(tile, cycle_shift, cycle_weight, cycle_scale, lens_weight):
    rows = tile.shape[0]
    entries = 2 * TAPS + 3 + lens_weight.shape[1] // 2
    return pl.pallas_call(
        prepare_kernel,
        out_shape=(
            jax.ShapeDtypeStruct((HALO, rows), jnp.float32),
            jax.ShapeDtypeStruct((HALO, rows), jnp.float32),
            jax.ShapeDtypeStruct((entries, 2, 8, rows // 2), jnp.float32),
        ),
        in_specs=[vmem()] * 5,
        out_specs=(vmem(),) * 3,
        cost_estimate=pl.CostEstimate(flops=1 << 16, bytes_accessed=1 << 20, transcendentals=0),
        name="prepare",
    )(tile, cycle_shift, cycle_weight, cycle_scale[None], lens_weight)


def per_device(potential, lens_weight, cycle_shift, cycle_weight, cycle_scale):
    tile = potential[0]
    rows, width = tile.shape
    lon, plane = lax.axis_index("lon"), lax.axis_index("plane")
    near_hi = (((plane // NX) * Z_LO + lon // RING + 1) // Z_LO) % Z_HI
    scalars = jnp.where(jnp.arange(2) == 0, plane % NX, near_hi).astype(jnp.int32)

    near, far = z_move(tile, 1), z_move(tile, 1 + Z_LO)
    low, high, tables = prepare(tile, cycle_shift, cycle_weight, cycle_scale, lens_weight)
    strips = jnp.concatenate([z_move(low, 1, -1), z_move(high, 1, 1)])
    near = jnp.concatenate([near, strips])
    near_tiles = [near] + [x_move(near, ahead) for ahead in NEAR[1:]]
    far = jnp.concatenate([far, swap(strips)])
    far_tiles = [far] + [x_move(far, ahead) for ahead in FAR[1:]]

    params = pltpu.CompilerParams(vmem_limit_bytes=24 << 20)
    state_shape = (6, 2, width, rows // 2)
    state = pl.pallas_call(
        near_kernel,
        out_shape=jax.ShapeDtypeStruct(state_shape, jnp.float32),
        in_specs=[smem()] + [vmem()] * 5,
        out_specs=vmem(),
        scratch_shapes=[
            pltpu.VMEM(ext_shape(NX, rows, width), jnp.float32),
            pltpu.VMEM(fields_shape(NX, rows, width), jnp.float32),
        ],
        cost_estimate=cost(NX, rows, width),
        compiler_params=params,
        name="near_planes",
    )(scalars, tables, *near_tiles)
    early = pl.pallas_call(
        early_kernel,
        out_shape=jax.ShapeDtypeStruct(fields_shape(NX - 1, rows, width), jnp.float32),
        in_specs=[vmem()] * NX + [pl.BlockSpec(memory_space=pl.ANY)],
        out_specs=vmem(),
        scratch_shapes=[pltpu.VMEM(ext_shape(NX - 1, rows, width), jnp.float32)],
        cost_estimate=cost(NX // 2, rows, width),
        compiler_params=params,
        name="far_planes_early",
    )(tables, *far_tiles[: NX - 1], state)
    displacement, jacobian = pl.pallas_call(
        far_kernel,
        out_shape=(
            jax.ShapeDtypeStruct((2, rows, width), jnp.float32),
            jax.ShapeDtypeStruct((4, rows, width), jnp.float32),
        ),
        in_specs=[smem()] + [vmem()] * 4,
        out_specs=(vmem(), vmem()),
        scratch_shapes=[
            pltpu.VMEM(ext_shape(1, rows, width), jnp.float32),
            pltpu.VMEM(fields_shape(1, rows, width), jnp.float32),
            pltpu.VMEM(state_shape, jnp.float32),
        ],
        cost_estimate=cost(NX, rows, width),
        compiler_params=params,
        name="far_planes",
    )(scalars, tables, far_tiles[NX - 1], early, state)
    return displacement[None], jacobian[None]


def solution(mesh):
    in_specs = (P("plane", None, "lon"), P("plane", None), P(), P(), P())
    out_specs = (P("plane", None, None, "lon"), P("plane", None, None, "lon"))
    return jax.shard_map(
        per_device, mesh=mesh, in_specs=in_specs, out_specs=out_specs, check_vma=False
    )
```

```python
import jax
import jax.numpy as jnp
from jax import lax
from jax.experimental import pallas as pl
from jax.experimental.pallas import tpu as pltpu
from jax.sharding import PartitionSpec as P

HALO = 4
TAPS = 7
PAD = 24
STEP = 48
BLOCK = 16
NEAR = (0, 1, 3, 2)
FAR = (0, 3, 2, 1)
Z_LO, Z_HI, NX, RING = 4, 2, 4, 16


def z_move(value, ahead, steps=0):
    pairs = []
    for z_lo in range(Z_LO):
        for z_hi in range(Z_HI):
            for ring in range(RING):
                for x in range(NX):
                    z = (z_hi * Z_LO + z_lo + ahead) % (Z_LO * Z_HI)
                    lon = (((z_lo + 1) % Z_LO) * RING + ring + steps) % (Z_LO * RING)
                    source = lon * Z_HI * NX + (z // Z_LO) * NX + x
                    target = (z_lo * RING + ring) * Z_HI * NX + z_hi * NX + x
                    pairs.append((source, target))
    return lax.ppermute(value, ("lon", "plane"), pairs)


def swap(value):
    pairs = [(z_hi * NX + x, (1 - z_hi) * NX + x) for z_hi in range(Z_HI) for x in range(NX)]
    return lax.ppermute(value, "plane", pairs)


def x_move(value, ahead):
    pairs = [
        (z_hi * NX + (x + ahead) % NX, z_hi * NX + x) for z_hi in range(Z_HI) for x in range(NX)
    ]
    return lax.ppermute(value, "plane", pairs)


def load_planes(slots, tiles, ext):
    for slot, tile in zip(slots, tiles):
        width = tile.shape[1]
        for half in range(2):
            rows = slice(half * 128, half * 128 + 128)
            ext[slot, half, PAD : PAD + width, :] = tile[rows, :].T
            ext[slot, half, PAD - HALO : PAD, :] = tile[width : width + HALO, rows]
            ext[slot, half, PAD + width : PAD + width + HALO, :] = tile[
                width + HALO : width + 2 * HALO, rows
            ]


def stencils(width, taps_ref, ext, fields):
    lane = lax.broadcasted_iota(jnp.int32, (STEP // 8, 8, 128), 2)
    first, last = lane == 0, lane == 127
    start = PAD - 16

    def step(i, carry):
        at = pl.multiple_of(start + i * STEP, 8)
        for slot in range(ext.shape[0]):
            norths, souths, centres = [], [], []
            for half in range(2):
                views = [
                    ext[slot, half, pl.ds(at + tap - 3, STEP), :].reshape(STEP // 8, 8, 128)
                    for tap in range(TAPS)
                ]
                north = views[0] * taps_ref[0, half]
                south = views[0] * taps_ref[TAPS, half]
                for tap in range(1, TAPS):
                    north += views[tap] * taps_ref[tap, half]
                    south += views[tap] * taps_ref[TAPS + tap, half]
                twice = views[3] + views[3]
                east, west = views[4], views[2]
                fields[slot, half, 2, pl.ds(at, STEP), :] = (east - west).reshape(STEP, 128)
                fields[slot, half, 3, pl.ds(at, STEP), :] = (east + west - twice).reshape(STEP, 128)
                norths.append(pltpu.roll(north.reshape(STEP, 128), 1, 1).reshape(north.shape))
                souths.append(pltpu.roll(south.reshape(STEP, 128), 127, 1).reshape(north.shape))
                centres.append(twice)
            n = [jnp.where(first, 0.0, norths[0]), jnp.where(first, norths[0], norths[1])]
            s = [jnp.where(last, souths[1], souths[0]), jnp.where(last, 0.0, souths[1])]
            for half in range(2):
                fields[slot, half, 0, pl.ds(at, STEP), :] = (s[half] - n[half]).reshape(STEP, 128)
                fields[slot, half, 1, pl.ds(at, STEP), :] = (
                    s[half] + n[half] - centres[half]
                ).reshape(STEP, 128)
        return carry

    lax.fori_loop(0, (width + 2 * 16) // STEP, step, 0)


def compose(half, hi, tables, load):
    half_m, square_m, quarter_m = [tables[2 * TAPS + k, half] for k in range(3)]
    state = None
    for slot in range(NX):
        gain = tables[2 * TAPS + 3 + hi * (NX // 2) + slot // 2, slot % 2]
        alpha_t = (0.5 * gain) * load(slot, 0)
        alpha_p = (gain * half_m) * load(slot, 2)
        u_tt = gain * load(slot, 1)
        u_pp = (gain * square_m) * load(slot, 3)
        u_tp = (gain * quarter_m) * (load(slot, 0, 1) - load(slot, 0, -1))
        if state is None:
            state = (-alpha_t, -alpha_p, 1.0 - u_tt, -u_tp, -u_tp, 1.0 - u_pp)
        else:
            d_t, d_p, a_zz, a_zo, a_oz, a_oo = state
            state = (
                d_t - (alpha_t + (u_tt * d_t + u_tp * d_p)),
                d_p - (alpha_p + (u_tp * d_t + u_pp * d_p)),
                a_zz - (u_tt * a_zz + u_tp * a_oz),
                a_zo - (u_tt * a_zo + u_tp * a_oo),
                a_oz - (u_tp * a_zz + u_pp * a_oz),
                a_oo - (u_tp * a_zo + u_pp * a_oo),
            )
    return state


def block_of(ref, at):
    return ref[pl.ds(at, BLOCK), :].reshape(BLOCK // 8, 8, 128)


def near_kernel(scalar_ref, tables, t0, t1, t2, t3, out, ext, fields):
    width = t0.shape[1]
    slots = [lax.rem(scalar_ref[0] + ahead, NX) for ahead in NEAR]
    load_planes(slots, (t0, t1, t2, t3), ext)
    stencils(width, tables, ext, fields)
    hi = scalar_ref[1]

    def block(j, carry):
        at = pl.multiple_of(j * BLOCK, BLOCK)
        for half in range(2):

            def load(slot, k, shift=0):
                return block_of(fields.at[slot, half, k], at + PAD + shift)

            state = compose(half, hi, tables, load)
            for k in range(6):
                out[k, half, pl.ds(at, BLOCK), :] = state[k].reshape(BLOCK, 128)
        return carry

    lax.fori_loop(0, width // BLOCK, block, 0)


def early_kernel(tables, t0, t1, t2, after, fields, ext):
    load_planes(range(3), (t0, t1, t2), ext)
    stencils(t0.shape[1], tables, ext, fields)


def far_kernel(
    scalar_ref, tables, last, early, other, disp, jac, ext, fields, done, stage, sems
):
    width = last.shape[1]
    load_planes(range(1), (last,), ext)
    stencils(width, tables, ext, fields)
    hi = 1 - scalar_ref[1]
    other_first = hi == 1

    def rays(x, part):
        def block(j, carry):
            at = pl.multiple_of(j * BLOCK, BLOCK)
            for half in range(2):

                def load(slot, k, shift=0):
                    tile = FAR.index((slot - x) % NX)
                    ref = fields.at[0] if tile == NX - 1 else early.at[tile]
                    return block_of(ref.at[half, k], at + PAD + shift)

                here = compose(half, hi, tables, load)
                there = [block_of(other.at[k, half], at) for k in range(6)]
                d_t, d_p, a_zz, a_zo, a_oz, a_oo = [
                    jnp.where(other_first, a, b) for a, b in zip(there, here)
                ]
                e_t, e_p, b_zz, b_zo, b_oz, b_oo = [
                    jnp.where(other_first, b, a) for a, b in zip(there, here)
                ]
                state = (
                    e_t + (b_zz * d_t + b_zo * d_p),
                    e_p + (b_oz * d_t + b_oo * d_p),
                    b_zz * a_zz + b_zo * a_oz,
                    b_zz * a_zo + b_zo * a_oo,
                    b_oz * a_zz + b_oo * a_oz,
                    b_oz * a_zo + b_oo * a_oo,
                )
                for k in range(6):
                    done[k, half, pl.ds(at, BLOCK), :] = state[k].reshape(BLOCK, 128)
            return carry

        count = width // BLOCK // 2
        lax.fori_loop(part * count, part * count + count, block, 0)

    copies = []
    for part in range(2):
        for x in range(NX):
            pl.when(scalar_ref[0] == x)(lambda x=x, part=part: rays(x, part))
        columns = slice(part * 128, part * 128 + 128)
        for k in range(6):
            for half in range(2):
                rows = slice(half * 128, half * 128 + 128)
                stage[k, rows, columns] = done[k, half, columns].T
            target = disp.at[k] if k < 2 else jac.at[k - 2]
            copy = pltpu.make_async_copy(
                stage.at[k, :, columns], target.at[:, columns], sems.at[part * 6 + k]
            )
            copy.start()
            copies.append(copy)
    for copy in copies:
        copy.wait()


def smem():
    return pl.BlockSpec(memory_space=pltpu.SMEM)


def vmem():
    return pl.BlockSpec(memory_space=pltpu.VMEM)


def ext_shape(count, rows, width):
    return (count, 2, width + 2 * PAD, rows // 2)


def fields_shape(count, rows, width):
    return (count, 2, 4, width + 2 * PAD, rows // 2)


def cost(planes, rows, width):
    return pl.CostEstimate(
        flops=260 * planes * rows * width, bytes_accessed=40 * rows * width, transcendentals=0
    )


def prepare_kernel(tile_ref, shift_ref, weight_ref, scale_ref, gain_ref, low, high, tables):
    rows, width = tile_ref.shape
    for half in range(2):
        lanes = slice(half * 128, half * 128 + 128)
        low[:, lanes] = tile_ref[lanes, width - 128 :].T[128 - HALO :]
        high[:, lanes] = tile_ref[lanes, :128].T[:HALO]
    for side, turn in ((0, rows - 1), (1, 1)):
        shift = jnp.broadcast_to(shift_ref[side : side + 1, :], (8, rows))
        frac = jnp.broadcast_to(weight_ref[side : side + 1, :].astype(jnp.float32) / 16.0, (8, rows))
        shift, frac = pltpu.roll(shift, turn, 1), pltpu.roll(frac, turn, 1)
        for tap in range(TAPS):
            value = jnp.where(shift == tap - 3, 1.0 - frac, 0.0)
            value += jnp.where(shift == tap - 4, frac, 0.0)
            for half in range(2):
                tables[side * TAPS + tap, half] = value[:, half * 128 : half * 128 + 128]
    scale = jnp.broadcast_to(scale_ref[...], (8, rows))
    for k, value in enumerate((0.5 * scale, scale * scale, 0.25 * scale)):
        for half in range(2):
            tables[2 * TAPS + k, half] = value[:, half * 128 : half * 128 + 128]
    for k in range(gain_ref.shape[1]):
        tables[2 * TAPS + 3 + k // 2, k % 2] = jnp.broadcast_to(gain_ref[:, k : k + 1], (8, rows // 2))


def prepare(tile, cycle_shift, cycle_weight, cycle_scale, lens_weight):
    rows = tile.shape[0]
    entries = 2 * TAPS + 3 + lens_weight.shape[1] // 2
    return pl.pallas_call(
        prepare_kernel,
        out_shape=(
            jax.ShapeDtypeStruct((HALO, rows), jnp.float32),
            jax.ShapeDtypeStruct((HALO, rows), jnp.float32),
            jax.ShapeDtypeStruct((entries, 2, 8, rows // 2), jnp.float32),
        ),
        in_specs=[vmem()] * 5,
        out_specs=(vmem(),) * 3,
        cost_estimate=pl.CostEstimate(flops=1 << 16, bytes_accessed=1 << 20, transcendentals=0),
        name="prepare",
    )(tile, cycle_shift, cycle_weight, cycle_scale[None], lens_weight)


def per_device(potential, lens_weight, cycle_shift, cycle_weight, cycle_scale):
    tile = potential[0]
    rows, width = tile.shape
    lon, plane = lax.axis_index("lon"), lax.axis_index("plane")
    near_hi = (((plane // NX) * Z_LO + lon // RING + 1) // Z_LO) % Z_HI
    scalars = jnp.where(jnp.arange(2) == 0, plane % NX, near_hi).astype(jnp.int32)

    near, far = z_move(tile, 1), z_move(tile, 1 + Z_LO)
    low, high, tables = prepare(tile, cycle_shift, cycle_weight, cycle_scale, lens_weight)
    strips = jnp.concatenate([z_move(low, 1, -1), z_move(high, 1, 1)])
    near = jnp.concatenate([near, strips])
    near_tiles = [near] + [x_move(near, ahead) for ahead in NEAR[1:]]
    far = jnp.concatenate([far, swap(strips)])
    far_tiles = [far] + [x_move(far, ahead) for ahead in FAR[1:]]

    params = pltpu.CompilerParams(vmem_limit_bytes=24 << 20)
    state_shape = (6, 2, width, rows // 2)
    state = pl.pallas_call(
        near_kernel,
        out_shape=jax.ShapeDtypeStruct(state_shape, jnp.float32),
        in_specs=[smem()] + [vmem()] * 5,
        out_specs=vmem(),
        scratch_shapes=[
            pltpu.VMEM(ext_shape(NX, rows, width), jnp.float32),
            pltpu.VMEM(fields_shape(NX, rows, width), jnp.float32),
        ],
        cost_estimate=cost(NX, rows, width),
        compiler_params=params,
        name="near_planes",
    )(scalars, tables, *near_tiles)
    early = pl.pallas_call(
        early_kernel,
        out_shape=jax.ShapeDtypeStruct(fields_shape(NX - 1, rows, width), jnp.float32),
        in_specs=[vmem()] * NX + [pl.BlockSpec(memory_space=pl.ANY)],
        out_specs=vmem(),
        scratch_shapes=[pltpu.VMEM(ext_shape(NX - 1, rows, width), jnp.float32)],
        cost_estimate=cost(NX // 2, rows, width),
        compiler_params=params,
        name="far_planes_early",
    )(tables, *far_tiles[: NX - 1], state)
    displacement, jacobian = pl.pallas_call(
        far_kernel,
        out_shape=(
            jax.ShapeDtypeStruct((2, rows, width), jnp.float32),
            jax.ShapeDtypeStruct((4, rows, width), jnp.float32),
        ),
        in_specs=[smem()] + [vmem()] * 4,
        out_specs=(pl.BlockSpec(memory_space=pl.ANY),) * 2,
        scratch_shapes=[
            pltpu.VMEM(ext_shape(1, rows, width), jnp.float32),
            pltpu.VMEM(fields_shape(1, rows, width), jnp.float32),
            pltpu.VMEM(state_shape, jnp.float32),
            pltpu.VMEM((6, rows, width), jnp.float32),
            pltpu.SemaphoreType.DMA((12,)),
        ],
        cost_estimate=cost(NX, rows, width),
        compiler_params=params,
        name="far_planes",
    )(scalars, tables, far_tiles[NX - 1], early, state)
    return displacement[None], jacobian[None]


def solution(mesh):
    in_specs = (P("plane", None, "lon"), P("plane", None), P(), P(), P())
    out_specs = (P("plane", None, None, "lon"), P("plane", None, None, "lon"))
    return jax.shard_map(
        per_device, mesh=mesh, in_specs=in_specs, out_specs=out_specs, check_vma=False
    )
```

```python
import jax
import jax.numpy as jnp
from jax import lax
from jax.experimental import pallas as pl
from jax.experimental.pallas import tpu as pltpu
from jax.sharding import PartitionSpec as P

HALO = 4
TAPS = 7
PAD = 24
STEP = 48
BLOCK = 16
NEAR = (0, 1, 3, 2)
FAR = (0, 3, 2, 1)
Z_LO, Z_HI, NX, RING = 4, 2, 4, 16


def z_move(value, ahead, steps=0):
    pairs = []
    for z_lo in range(Z_LO):
        for z_hi in range(Z_HI):
            for ring in range(RING):
                for x in range(NX):
                    z = (z_hi * Z_LO + z_lo + ahead) % (Z_LO * Z_HI)
                    lon = (((z_lo + 1) % Z_LO) * RING + ring + steps) % (Z_LO * RING)
                    source = lon * Z_HI * NX + (z // Z_LO) * NX + x
                    target = (z_lo * RING + ring) * Z_HI * NX + z_hi * NX + x
                    pairs.append((source, target))
    return lax.ppermute(value, ("lon", "plane"), pairs)


def swap(value):
    pairs = [(z_hi * NX + x, (1 - z_hi) * NX + x) for z_hi in range(Z_HI) for x in range(NX)]
    return lax.ppermute(value, "plane", pairs)


def x_move(value, ahead):
    pairs = [
        (z_hi * NX + (x + ahead) % NX, z_hi * NX + x) for z_hi in range(Z_HI) for x in range(NX)
    ]
    return lax.ppermute(value, "plane", pairs)


def load_planes(slots, tiles, ext):
    for slot, tile in zip(slots, tiles):
        width = tile.shape[1]
        for half in range(2):
            rows = slice(half * 128, half * 128 + 128)
            ext[slot, half, PAD : PAD + width, :] = tile[rows, :].T
            ext[slot, half, PAD - HALO : PAD, :] = tile[width : width + HALO, rows]
            ext[slot, half, PAD + width : PAD + width + HALO, :] = tile[
                width + HALO : width + 2 * HALO, rows
            ]


def stencils(width, taps_ref, ext, fields):
    lane = lax.broadcasted_iota(jnp.int32, (STEP // 8, 8, 128), 2)
    first, last = lane == 0, lane == 127
    start = PAD - 16

    def step(i, carry):
        at = pl.multiple_of(start + i * STEP, 8)
        for slot in range(ext.shape[0]):
            norths, souths, centres = [], [], []
            for half in range(2):
                views = [
                    ext[slot, half, pl.ds(at + tap - 3, STEP), :].reshape(STEP // 8, 8, 128)
                    for tap in range(TAPS)
                ]
                north = views[0] * taps_ref[0, half]
                south = views[0] * taps_ref[TAPS, half]
                for tap in range(1, TAPS):
                    north += views[tap] * taps_ref[tap, half]
                    south += views[tap] * taps_ref[TAPS + tap, half]
                twice = views[3] + views[3]
                east, west = views[4], views[2]
                fields[slot, half, 2, pl.ds(at, STEP), :] = (east - west).reshape(STEP, 128)
                fields[slot, half, 3, pl.ds(at, STEP), :] = (east + west - twice).reshape(STEP, 128)
                norths.append(pltpu.roll(north.reshape(STEP, 128), 1, 1).reshape(north.shape))
                souths.append(pltpu.roll(south.reshape(STEP, 128), 127, 1).reshape(north.shape))
                centres.append(twice)
            n = [jnp.where(first, 0.0, norths[0]), jnp.where(first, norths[0], norths[1])]
            s = [jnp.where(last, souths[1], souths[0]), jnp.where(last, 0.0, souths[1])]
            for half in range(2):
                fields[slot, half, 0, pl.ds(at, STEP), :] = (s[half] - n[half]).reshape(STEP, 128)
                fields[slot, half, 1, pl.ds(at, STEP), :] = (
                    s[half] + n[half] - centres[half]
                ).reshape(STEP, 128)
        return carry

    lax.fori_loop(0, (width + 2 * 16) // STEP, step, 0)


def compose(half, hi, tables, load):
    half_m, square_m, quarter_m = [tables[2 * TAPS + k, half] for k in range(3)]
    state = None
    for slot in range(NX):
        gain = tables[2 * TAPS + 3 + hi * (NX // 2) + slot // 2, slot % 2]
        alpha_t = (0.5 * gain) * load(slot, 0)
        alpha_p = (gain * half_m) * load(slot, 2)
        u_tt = gain * load(slot, 1)
        u_pp = (gain * square_m) * load(slot, 3)
        u_tp = (gain * quarter_m) * (load(slot, 0, 1) - load(slot, 0, -1))
        if state is None:
            state = (-alpha_t, -alpha_p, 1.0 - u_tt, -u_tp, -u_tp, 1.0 - u_pp)
        else:
            d_t, d_p, a_zz, a_zo, a_oz, a_oo = state
            state = (
                d_t - (alpha_t + (u_tt * d_t + u_tp * d_p)),
                d_p - (alpha_p + (u_tp * d_t + u_pp * d_p)),
                a_zz - (u_tt * a_zz + u_tp * a_oz),
                a_zo - (u_tt * a_zo + u_tp * a_oo),
                a_oz - (u_tp * a_zz + u_pp * a_oz),
                a_oo - (u_tp * a_zo + u_pp * a_oo),
            )
    return state


def block_of(ref, at):
    return ref[pl.ds(at, BLOCK), :].reshape(BLOCK // 8, 8, 128)


def near_kernel(scalar_ref, tables, t0, t1, t2, t3, out, ext, fields):
    width = t0.shape[1]
    slots = [lax.rem(scalar_ref[0] + ahead, NX) for ahead in NEAR]
    load_planes(slots, (t0, t1, t2, t3), ext)
    stencils(width, tables, ext, fields)
    hi = scalar_ref[1]

    def block(j, carry):
        at = pl.multiple_of(j * BLOCK, BLOCK)
        for half in range(2):

            def load(slot, k, shift=0):
                return block_of(fields.at[slot, half, k], at + PAD + shift)

            state = compose(half, hi, tables, load)
            for k in range(6):
                out[k, half, pl.ds(at, BLOCK), :] = state[k].reshape(BLOCK, 128)
        return carry

    lax.fori_loop(0, width // BLOCK, block, 0)


def early_kernel(tables, t0, t1, t2, after, fields, ext):
    load_planes(range(3), (t0, t1, t2), ext)
    stencils(t0.shape[1], tables, ext, fields)


def far_kernel(scalar_ref, tables, last, early, other, disp, jac, ext, fields, done):
    width = last.shape[1]
    load_planes(range(1), (last,), ext)
    stencils(width, tables, ext, fields)
    hi = 1 - scalar_ref[1]
    other_first = hi == 1

    def rays(x):
        def block(j, carry):
            at = pl.multiple_of(j * BLOCK, BLOCK)
            for half in range(2):

                def load(slot, k, shift=0):
                    tile = FAR.index((slot - x) % NX)
                    ref = fields.at[0] if tile == NX - 1 else early.at[tile]
                    return block_of(ref.at[half, k], at + PAD + shift)

                here = compose(half, hi, tables, load)
                there = [block_of(other.at[k, half], at) for k in range(6)]
                d_t, d_p, a_zz, a_zo, a_oz, a_oo = [
                    jnp.where(other_first, a, b) for a, b in zip(there, here)
                ]
                e_t, e_p, b_zz, b_zo, b_oz, b_oo = [
                    jnp.where(other_first, b, a) for a, b in zip(there, here)
                ]
                state = (
                    e_t + (b_zz * d_t + b_zo * d_p),
                    e_p + (b_oz * d_t + b_oo * d_p),
                    b_zz * a_zz + b_zo * a_oz,
                    b_zz * a_zo + b_zo * a_oo,
                    b_oz * a_zz + b_oo * a_oz,
                    b_oz * a_zo + b_oo * a_oo,
                )
                for k in range(6):
                    done[k, half, pl.ds(at, BLOCK), :] = state[k].reshape(BLOCK, 128)
            return carry

        lax.fori_loop(0, width // BLOCK, block, 0)

    for x in range(NX):
        pl.when(scalar_ref[0] == x)(lambda x=x: rays(x))
    for k in range(6):
        for half in range(2):
            rows = slice(half * 128, half * 128 + 128)
            turned = done[k, half].T
            if k < 2:
                disp[k, rows, :] = turned
            else:
                jac[k - 2, rows, :] = turned


def smem():
    return pl.BlockSpec(memory_space=pltpu.SMEM)


def vmem():
    return pl.BlockSpec(memory_space=pltpu.VMEM)


def ext_shape(count, rows, width):
    return (count, 2, width + 2 * PAD, rows // 2)


def fields_shape(count, rows, width):
    return (count, 2, 4, width + 2 * PAD, rows // 2)


def cost(planes, rows, width):
    return pl.CostEstimate(
        flops=260 * planes * rows * width, bytes_accessed=40 * rows * width, transcendentals=0
    )


def prepare_kernel(tile_ref, shift_ref, weight_ref, scale_ref, gain_ref, low, high, tables):
    rows, width = tile_ref.shape
    for half in range(2):
        lanes = slice(half * 128, half * 128 + 128)
        low[:, lanes] = tile_ref[lanes, width - 128 :].T[128 - HALO :]
        high[:, lanes] = tile_ref[lanes, :128].T[:HALO]
    for side, turn in ((0, rows - 1), (1, 1)):
        shift = jnp.broadcast_to(shift_ref[side : side + 1, :], (8, rows))
        frac = jnp.broadcast_to(weight_ref[side : side + 1, :].astype(jnp.float32) / 16.0, (8, rows))
        shift, frac = pltpu.roll(shift, turn, 1), pltpu.roll(frac, turn, 1)
        for tap in range(TAPS):
            value = jnp.where(shift == tap - 3, 1.0 - frac, 0.0)
            value += jnp.where(shift == tap - 4, frac, 0.0)
            for half in range(2):
                tables[side * TAPS + tap, half] = value[:, half * 128 : half * 128 + 128]
    scale = jnp.broadcast_to(scale_ref[...], (8, rows))
    for k, value in enumerate((0.5 * scale, scale * scale, 0.25 * scale)):
        for half in range(2):
            tables[2 * TAPS + k, half] = value[:, half * 128 : half * 128 + 128]
    for k in range(gain_ref.shape[1]):
        tables[2 * TAPS + 3 + k // 2, k % 2] = jnp.broadcast_to(gain_ref[:, k : k + 1], (8, rows // 2))


def prepare(tile, cycle_shift, cycle_weight, cycle_scale, lens_weight):
    rows = tile.shape[0]
    entries = 2 * TAPS + 3 + lens_weight.shape[1] // 2
    return pl.pallas_call(
        prepare_kernel,
        out_shape=(
            jax.ShapeDtypeStruct((HALO, rows), jnp.float32),
            jax.ShapeDtypeStruct((HALO, rows), jnp.float32),
            jax.ShapeDtypeStruct((entries, 2, 8, rows // 2), jnp.float32),
        ),
        in_specs=[vmem()] * 5,
        out_specs=(vmem(),) * 3,
        cost_estimate=pl.CostEstimate(flops=1 << 16, bytes_accessed=1 << 20, transcendentals=0),
        name="prepare",
    )(tile, cycle_shift, cycle_weight, cycle_scale[None], lens_weight)


def per_device(potential, lens_weight, cycle_shift, cycle_weight, cycle_scale):
    tile = potential[0]
    rows, width = tile.shape
    lon, plane = lax.axis_index("lon"), lax.axis_index("plane")
    near_hi = (((plane // NX) * Z_LO + lon // RING + 1) // Z_LO) % Z_HI
    scalars = jnp.where(jnp.arange(2) == 0, plane % NX, near_hi).astype(jnp.int32)

    near, far = z_move(tile, 1), z_move(tile, 1 + Z_LO)
    low, high, tables = prepare(tile, cycle_shift, cycle_weight, cycle_scale, lens_weight)
    strips = jnp.concatenate([z_move(low, 1, -1), z_move(high, 1, 1)])
    near = jnp.concatenate([near, strips])
    near_tiles = [near] + [x_move(near, ahead) for ahead in NEAR[1:]]
    far = jnp.concatenate([far, swap(strips)])
    across, far = lax.optimization_barrier((near_tiles[NEAR.index(2)], far))
    far_tiles = [far] + [swap(across) if ahead == 2 else x_move(far, ahead) for ahead in FAR[1:]]

    params = pltpu.CompilerParams(vmem_limit_bytes=24 << 20)
    state_shape = (6, 2, width, rows // 2)
    state = pl.pallas_call(
        near_kernel,
        out_shape=jax.ShapeDtypeStruct(state_shape, jnp.float32),
        in_specs=[smem()] + [vmem()] * 5,
        out_specs=vmem(),
        scratch_shapes=[
            pltpu.VMEM(ext_shape(NX, rows, width), jnp.float32),
            pltpu.VMEM(fields_shape(NX, rows, width), jnp.float32),
        ],
        cost_estimate=cost(NX, rows, width),
        compiler_params=params,
        name="near_planes",
    )(scalars, tables, *near_tiles)
    early = pl.pallas_call(
        early_kernel,
        out_shape=jax.ShapeDtypeStruct(fields_shape(NX - 1, rows, width), jnp.float32),
        in_specs=[vmem()] * NX + [pl.BlockSpec(memory_space=pl.ANY)],
        out_specs=vmem(),
        scratch_shapes=[pltpu.VMEM(ext_shape(NX - 1, rows, width), jnp.float32)],
        cost_estimate=cost(NX // 2, rows, width),
        compiler_params=params,
        name="far_planes_early",
    )(tables, *far_tiles[: NX - 1], state)
    displacement, jacobian = pl.pallas_call(
        far_kernel,
        out_shape=(
            jax.ShapeDtypeStruct((2, rows, width), jnp.float32),
            jax.ShapeDtypeStruct((4, rows, width), jnp.float32),
        ),
        in_specs=[smem()] + [vmem()] * 4,
        out_specs=(vmem(), vmem()),
        scratch_shapes=[
            pltpu.VMEM(ext_shape(1, rows, width), jnp.float32),
            pltpu.VMEM(fields_shape(1, rows, width), jnp.float32),
            pltpu.VMEM(state_shape, jnp.float32),
        ],
        cost_estimate=cost(NX, rows, width),
        compiler_params=params,
        name="far_planes",
    )(scalars, tables, far_tiles[NX - 1], early, state)
    return displacement[None], jacobian[None]


def solution(mesh):
    in_specs = (P("plane", None, "lon"), P("plane", None), P(), P(), P())
    out_specs = (P("plane", None, None, "lon"), P("plane", None, None, "lon"))
    return jax.shard_map(
        per_device, mesh=mesh, in_specs=in_specs, out_specs=out_specs, check_vma=False
    )
```
